1024 devices in a mesh: dp: 128 (over z, x, core), tensor: 8 (over y).
Axes of the slice: x: 4, y: 8, z: 16, core: 2. Of those that a mesh axis runs over, the one named last changes fastest.
Arguments:
- activations: bfloat16 [24576, 8192], P('dp'), may hold values from -6 to 6
- out_grads: bfloat16 [24576, 2048], P('dp', 'tensor'), may hold values from -6 to 6
- kv_weight: bfloat16 [8192, 2048], P('dp', 'tensor'), may hold values from -0.125 to 0.125
- block_ids: int32 [8, 6], P('tensor'), may hold values from 0 to 127, as said below
- block_owner: int32 [8, 6], P('tensor'), may hold values from 0 to 127, as said below
Outputs:
- input_grad: bfloat16 [24576, 8192], P('dp', 'tensor')
- owned_grads: float32 [8, 256, 128, 128], P('tensor', 'dp')
The draws below stay inside these ranges and needn't reach their ends.
Inputs may be any that keep to these rules, and one draw needn't show every extreme that they name: `block_ids`: within one shard the 6 block numbers are distinct. `block_owner`: within one shard no owner holds more than 2 blocks, and some owner holds exactly 2.
All inputs are finite; a program needn't handle non-finite values.
Results may differ from the reference program's by a relative error of at most 0.001.
Values may be sent and summed in bfloat16 or wider, within the bound.
A program may use at most 32 MiB of HBM per device.

```python
import jax
import jax.numpy as jnp
from jax import lax

D = 8192
KVC = 2048
BLK = 128
NB = 6
CAP = 2
TOKENS = 24576
SHARDS = 8
OWNERS = 128
ROWBLK = 64
COLBLK = 2


def draw_block_ids(key, part):

    def one_shard(index):
        return jax.random.permutation(jax.random.fold_in(key, index), ROWBLK * COLBLK)[:NB]
    return jax.vmap(one_shard)(jnp.arange(SHARDS)).astype(jnp.int32)


def draw_block_owner(key, part):

    def one_shard(index):
        first_key = jax.random.fold_in(key, 1000 + index)
        second_key = jax.random.fold_in(key, 5000 + index)
        picked = jax.random.permutation(first_key, OWNERS)[:NB]
        places = jax.random.permutation(second_key, NB)
        return picked.at[places[1]].set(picked[places[0]])
    return jax.vmap(one_shard)(jnp.arange(SHARDS)).astype(jnp.int32)


def block_levels(key, extent, pieces, low, top_value):
    def one(dim, shards_of):
        heights = jax.random.uniform(jax.random.fold_in(jax.random.fold_in(key, 6), dim), (shards_of,), jnp.float32, low / len(pieces), top_value / len(pieces))
        return jnp.repeat(jnp.exp(heights), extent[dim] // shards_of).reshape((-1,) + (1,) * (len(extent) - dim - 1))

    factor_of = one(*pieces[0])
    for cut in pieces[1:]:
        factor_of = factor_of * one(*cut)
    return factor_of


def gaussian(key, shape, spread, reach, pieces=(), kind=jnp.bfloat16):
    values = jax.random.normal(key, shape, jnp.float32) * spread
    if len(pieces) > 0:
        values = block_levels(key, shape, pieces, -0.22, 0.18) * values
    return jnp.clip(values, min=-reach, max=reach).astype(kind)


def setup_inputs(seed: int = 0) -> dict:
    key_list = jax.random.split(jax.random.key(seed), 6)
    activations = gaussian(key_list[0], (TOKENS, D), 1.0, 6.0, ((0, 128),))
    out_grads = gaussian(key_list[1], (TOKENS, KVC), 1.0, 6.0, ((0, 128), (1, 8)))
    kv_weight = gaussian(key_list[2], (D, KVC), KVC ** -0.5, 0.125, ((0, 128), (1, 8)))
    block_ids = draw_block_ids(jax.random.fold_in(key_list[5], 71), 0)
    block_owner = draw_block_owner(jax.random.fold_in(key_list[5], 71), 0)
    return dict(activations=activations, out_grads=out_grads, kv_weight=kv_weight, block_ids=block_ids, block_owner=block_owner)


def reference(activations, out_grads, kv_weight, block_ids, block_owner):
    shard_cols = KVC // SHARDS
    input_grad = lax.dot_general(out_grads, kv_weight, (((1,), (1,)), ((), ())), preferred_element_type=jnp.float32).astype(jnp.bfloat16)

    x_split = activations.reshape(TOKENS, ROWBLK, BLK)
    all_sums = []
    for group in range(SHARDS):
        numbers = block_ids[group]
        row_index = numbers // COLBLK
        col_index = numbers % COLBLK
        x_blocks = x_split[:, row_index, :].astype(jnp.float32)
        grads_group = out_grads[:, group * shard_cols:(group + 1) * shard_cols].reshape(TOKENS, COLBLK, BLK)
        g_blocks = grads_group[:, col_index, :].astype(jnp.float32)
        all_sums.append(jnp.einsum("tnb,tnc->nbc", x_blocks, g_blocks, precision=lax.Precision.HIGHEST))
    block_sums = jnp.stack(all_sums)

    position = jnp.arange(NB, dtype=jnp.int32)
    same_owner = block_owner[:, :, None] == block_owner[:, None, :]
    before = position[None, None, :] < position[None, :, None]
    ranks = jnp.sum((same_owner & before).astype(jnp.int32), axis=2).astype(jnp.int32)
    slot_index = (block_owner * CAP + ranks).astype(jnp.int32)
    slot_range = jnp.arange(OWNERS * CAP, dtype=jnp.int32)
    one_hot = (slot_index[:, :, None] == slot_range[None, None, :]).astype(jnp.float32)
    owned_grads = jnp.einsum("tjm,tjbc->tmbc", one_hot, block_sums, precision=lax.Precision.HIGHEST)
    owned_grads = owned_grads * (float(TOKENS) ** -0.5)
    return input_grad, owned_grads
```

```python
import jax
import jax.numpy as jnp
from jax import lax
from jax.experimental import pallas as pl
from jax.experimental.pallas import tpu as pltpu
from jax.sharding import PartitionSpec as P

MESH = pl.DeviceIdType.MESH
NX, NY, NZ = 4, 8, 16
BLK = 128
NB = 6
CAP = 2
PIECES = 12
SCALE = 24576.0 ** -0.5


def block_terms(ids_ref, owner_ref, x_hbm, g_hbm, part_ref, sel_ref, xbuf, gbuf, sems):
    dp = lax.axis_index("dp")
    c, x, z = dp % 2, (dp // 2) % NX, dp // 8
    copies = [pltpu.make_async_copy(g_hbm, gbuf, sems.at[NB])]
    for n in range(NB):
        rows = pl.multiple_of((ids_ref[0, n] // 2) * BLK, BLK)
        copies.append(pltpu.make_async_copy(x_hbm.at[:, pl.ds(rows, BLK)], xbuf.at[n], sems.at[n]))
    for copy in copies:
        copy.start()
    owners = [owner_ref[0, n] for n in range(NB)]
    ranks = []
    for n in range(NB):
        r = jnp.int32(0)
        for m in range(n):
            r = r + (owners[m] == owners[n]).astype(jnp.int32)
        ranks.append(r)
    for i in range(8):
        to = (z * NX + (x + i // 2) % NX) * 2 + (c + i % 2) % 2
        for s in range(CAP):
            for n in range(NB):
                hit = (owners[n] == to) & (ranks[n] == s)
                sel_ref[0, (i * CAP + s) * NB + n] = jnp.where(hit, jnp.float32(1), jnp.float32(0))
    copies[0].wait()
    for n in range(NB):
        copies[n + 1].wait()
        gb = gbuf[:, pl.ds(pl.multiple_of((ids_ref[0, n] % 2) * BLK, BLK), BLK)]
        term = lax.dot_general(
            xbuf[n], gb, (((0,), (0,)), ((), ())), preferred_element_type=jnp.float32
        )
        part_ref[0, n] = term[:64]
        part_ref[1, n] = term[64:]


def kernel(
    sel_ref, part_hbm, g_hbm, w_hbm, out_ref, owned_ref,
    wbuf, wown, gbuf, acc, part, half, xsum, xrecv, zsum, zrecv, mine, full, pick, got,
    load_sem, shard_ss, zs, xs, rs, cs, gs, as_, zr, xr, xl, x2, cr, gr, ar,
):
    dp = lax.axis_index("dp")
    y = lax.axis_index("tensor")
    c = dp % 2
    x = (dp // 2) % NX
    z = dp // 8
    role = (z - 2 * y + NZ) % NZ
    hown = role % 2
    slab = role < 2
    xp, xm, xo = (x + 1) % NX, (x + 3) % NX, (x + 2) % NX

    def dev(xx, yy, zz, cc):
        return ((zz * NX + xx) * 2 + cc, yy)

    def col(xx, hh, cc):
        return pl.multiple_of(hh * 512 + xx * 128 + cc * 64, 64)

    def unit(j, xx, hh, cc):
        return wbuf.at[j, pl.ds(col(xx, hh, cc), 64), :]

    def send(src, dst, ssem, rsem, to):
        pltpu.make_async_remote_copy(
            src_ref=src, dst_ref=dst, send_sem=ssem, recv_sem=rsem, device_id=to, device_id_type=MESH
        ).start()

    def desc(ref, ssem, rsem):
        return pltpu.make_async_remote_copy(
            src_ref=ref, dst_ref=ref, send_sem=ssem, recv_sem=rsem,
            device_id=dev(x, y, z, 1 - c), device_id_type=MESH,
        )

    def wait_recv(ref, rsem):
        desc(ref, cs, rsem).wait_recv()

    def wait_send(ref, ssem):
        desc(ref, ssem, gr).wait_send()

    load_p = pltpu.make_async_copy(part_hbm.at[c], part, load_sem.at[0])
    load_g = pltpu.make_async_copy(g_hbm, gbuf.at[y], load_sem.at[1])
    load_w = pltpu.make_async_copy(w_hbm, wown, load_sem.at[2])
    load_w.start()
    load_g.start()
    load_p.start()
    local_w = pltpu.make_async_copy(w_hbm, unit(0, x, hown, c), load_sem.at[3])

    @pl.when(slab)
    def _():
        local_w.start()

    barrier = pltpu.get_barrier_semaphore()
    peers = [dev(x, (y + i) % NY, z, c) for i in range(1, NY)]
    peers += [dev(x, y, (z + i) % NZ, c) for i in range(1, NZ)]
    peers += [dev((x + i) % NX, y, z, c) for i in range(1, NX)]
    peers += [dev((x + i) % NX, y, z, 1 - c) for i in range(NX)]
    for p in peers:
        pl.semaphore_signal(barrier, inc=1, device_id=p, device_id_type=MESH)

    load_g.wait()
    load_p.wait()
    load_w.wait()
    pl.semaphore_wait(barrier, len(peers))

    yd = z // 2
    d = (y - yd + NY) % NY
    jd = jnp.where(d == 0, 0, jnp.where(d <= 4, 2 * d - 1, 16 - 2 * d))

    @pl.when(jnp.logical_not(slab))
    def _():
        send(wown, unit(jd, x, hown, c), shard_ss, zr.at[2 * jd + z % 2], dev(x, yd, z, c))

    send(part_hbm.at[1 - c], half, as_.at[0], ar.at[0], dev(x, y, z, 1 - c))

    def spread(j, h, order):
        u = unit(j, x, h, c)
        k = 2 * j + h
        source = slab & (h == hown)
        up = jnp.where(
            role == 0, 1, jnp.where(role == 1, 4, 1)
        )
        down = jnp.where(role == 0, -4, jnp.where(role == 1, -1, -1))
        go_up = source | ((role >= 5) & (role <= 7)) | ((role >= 12) & (role <= 14))
        go_down = source | ((role >= 3) & (role <= 5)) | ((role >= 10) & (role <= 12))

        @pl.when(go_up)
        def _():
            send(u, u, zs, zr.at[k], dev(x, y, (z + up + NZ) % NZ, c))

        @pl.when(go_down)
        def _():
            send(u, u, zs, zr.at[k], dev(x, y, (z + down + NZ) % NZ, c))

        @pl.when(source)
        def _():
            far = jnp.where(role == 0, 5, -5)
            send(u, u, zs, zr.at[k], dev(x, y, (z + far + NZ) % NZ, c))

        send(u, u, xs, xr.at[j], dev(xp, y, z, c))
        send(u, u, xs, xl.at[j], dev(xm, y, z, c))
        send(u, u, cs, cr.at[j], dev(x, y, z, 1 - c))

    def take(j, h):
        wait_recv(unit(j, x, h, c), zr.at[2 * j + h])
        spread(j, h, 0)

    def core_step():
        wait_recv(half, ar.at[0])
        s = part[...] + half[...]
        for i in range(NX):
            xsum[i] = s[:, 16 * i:16 * (i + 1), :]
        for i in range(1, NX):
            xx = (x + i) % NX
            send(xsum.at[xx], xrecv.at[x], as_.at[1], ar.at[1], dev(xx, y, z, c))
        xrecv[x] = xsum[x]

    def x_step():
        wait_recv(xrecv.at[pl.ds(0, 3)], ar.at[1])
        s = xrecv[0] + xrecv[1] + xrecv[2] + xrecv[3]
        zsum[...] = s.reshape(PIECES, 8, 128)

        def body(i, carry):
            @pl.when(i != z)
            def _():
                send(zsum.at[i], zrecv.at[z], as_.at[2], ar.at[2], dev(x, y, i, c))

            return carry

        lax.fori_loop(0, PIECES, body, 0)

    def z_step():
        @pl.when(z < PIECES)
        def _():
            zrecv[z] = zsum[jnp.minimum(z, PIECES - 1)]
            wait_recv(zrecv.at[pl.ds(0, NZ - 1)], ar.at[2])
            s = zrecv[0]
            for i in range(1, NZ):
                s = s + zrecv[i]
            mine[...] = s * SCALE
            full[jnp.minimum(z, PIECES - 1)] = s * SCALE

            def body(i, carry):
                zz = (z + i) % NZ
                send(mine, full.at[jnp.minimum(z, PIECES - 1)], as_.at[3], ar.at[3], dev(x, y, zz, c))
                return carry

            lax.fori_loop(1, NZ, body, 0)

    def send_g():
        for i in (1, 7, 2, 6, 3, 5, 4):
            send(gbuf.at[y], gbuf.at[y], gs, gr, dev(x, (y + i) % NY, z, c))

    @pl.when(slab)
    def _():
        local_w.wait()
        spread(0, hown, 0)
        core_step()
        take(1, hown)
        take(2, hown)
        x_step()
        send_g()

        def body(j, carry):
            take(j, hown)
            return carry

        lax.fori_loop(3, 8, body, 0)

        def body2(j, carry):
            take(j, 1 - hown)
            return carry

        lax.fori_loop(0, 8, body2, 0)
        z_step()

    dist = jnp.where(role >= 9, jnp.abs(role - 12), jnp.abs(role - 5))
    jz = jnp.where(dist == 0, 5, jnp.where(dist == 1, 4, jnp.where(dist == 2, 2, 1)))

    @pl.when(jnp.logical_not(slab))
    def _():
        core_step()
        x_step()
        send_g()

        def body(j, carry):
            @pl.when(j == jz)
            def _():
                z_step()

            take(j, 0)
            take(j, 1)
            return carry

        lax.fori_loop(0, 8, body, 0)

    def body(j, carry):
        wait_recv(wbuf.at[j, pl.ds(0, 128), :], xr.at[j])
        even = j % 2 == 0
        for h in range(2):
            u = unit(j, xm, h, c)

            @pl.when(even)
            def _():
                send(u, u, rs, x2.at[j], dev(xp, y, z, c))

            send(u, u, cs, cr.at[j], dev(x, y, z, 1 - c))
        wait_recv(wbuf.at[j, pl.ds(0, 128), :], xl.at[j])
        for h in range(2):
            u = unit(j, xp, h, c)

            @pl.when(jnp.logical_not(even))
            def _():
                send(u, u, rs, x2.at[j], dev(xm, y, z, c))

            send(u, u, cs, cr.at[j], dev(x, y, z, 1 - c))
        return carry

    lax.fori_loop(0, 8, body, 0)

    @pl.when(z < PIECES)
    def _():
        wait_recv(full.at[pl.ds(0, PIECES - 1)], ar.at[3])

    @pl.when(z >= PIECES)
    def _():
        wait_recv(full, ar.at[3])

    row0 = pl.multiple_of(c * 64 + x * 16, 16)
    for i in range(8):
        xx, cc = (x + i // 2) % NX, (c + i % 2) % 2
        to = (z * NX + xx) * 2 + cc
        for s in range(CAP):
            total = jnp.zeros((2, 8, 128), jnp.float32)
            for n in range(NB):
                total = total + full[pl.ds(2 * n, 2)] * sel_ref[0, (i * CAP + s) * NB + n]
            if i == 0:
                got[s, pl.ds(row0, 16), :] = total.reshape(16, 128)
            else:
                pick[i - 1, s] = total.reshape(16, 128)
        if i > 0:
            send(pick.at[i - 1], got.at[:, pl.ds(row0, 16), :], as_.at[4], ar.at[4], (to, y))

    wait_recv(gbuf.at[pl.ds(0, 7)], gr)

    def product(j):
        shift = ((j + 1) // 2) * (2 * (j % 2) - 1)
        yw = (y + shift + NY) % NY
        wait_recv(wbuf.at[j, pl.ds(0, 512), :], cr.at[j])
        return lax.dot_general(
            gbuf[yw], wbuf[j], (((1,), (1,)), ((), ())), preferred_element_type=jnp.float32
        )

    def fetch(j):
        wait_recv(wbuf.at[j, pl.ds(0, 128), :], x2.at[j])
        for h in range(2):
            u = unit(j, xo, h, c)
            send(u, u, cs, cr.at[j], dev(x, y, z, 1 - c))

    acc[...] = jnp.zeros_like(acc)
    fetch(0)

    def body(j, carry):
        fetch(j)
        acc[...] += product(j - 1)
        return carry

    lax.fori_loop(1, 8, body, 0)
    out_ref[...] = (acc[...] + product(7)).astype(jnp.bfloat16)

    wait_recv(got.at[:, pl.ds(0, 112), :], ar.at[4])
    owned_ref[0] = got[...]

    @pl.when(jnp.logical_not(slab))
    def _():
        wait_send(wown, shard_ss)

    @pl.when(slab)
    def _():
        wait_send(wbuf.at[pl.ds(0, 3), pl.ds(0, 512), :], zs)

    @pl.when((role == 5) | (role == 12))
    def _():
        wait_send(wbuf.at[pl.ds(0, 2)], zs)

    @pl.when(
        (role == 3) | (role == 4) | (role == 6) | (role == 7)
        | (role == 10) | (role == 11) | (role == 13) | (role == 14)
    )
    def _():
        wait_send(wbuf.at[pl.ds(0, 1)], zs)

    wait_send(wbuf.at[pl.ds(0, 2)], xs)
    wait_send(wbuf.at[pl.ds(0, 1)], rs)
    wait_send(wbuf.at[pl.ds(0, 4)], cs)
    wait_send(gbuf.at[pl.ds(0, 7)], gs)
    wait_send(half, as_.at[0])
    wait_send(xsum.at[pl.ds(0, 3)], as_.at[1])

    @pl.when(z < PIECES)
    def _():
        wait_send(zsum.at[pl.ds(0, PIECES - 1)], as_.at[2])
        wait_send(zrecv.at[pl.ds(0, NZ - 1)], as_.at[3])

    @pl.when(z >= PIECES)
    def _():
        wait_send(zsum, as_.at[2])

    wait_send(pick, as_.at[4])


def local(activations, out_grads, kv_weight, block_ids, block_owner):
    f32, bf16 = jnp.float32, jnp.bfloat16
    dma = pltpu.SemaphoreType.DMA
    any_space = pl.BlockSpec(memory_space=pl.ANY)
    smem = pl.BlockSpec(memory_space=pltpu.SMEM)
    vmem = pl.BlockSpec(memory_space=pltpu.VMEM)
    part, sel = pl.pallas_call(
        block_terms,
        name="block_terms",
        out_shape=(
            jax.ShapeDtypeStruct((2, NB, 64, BLK), f32),
            jax.ShapeDtypeStruct((1, 8 * CAP * NB), f32),
        ),
        in_specs=[smem] * 2 + [any_space] * 2,
        out_specs=(vmem, smem),
        scratch_shapes=[
            pltpu.VMEM((NB, 192, BLK), bf16),
            pltpu.VMEM((192, 256), bf16),
            dma((NB + 1,)),
        ],
    )(block_ids, block_owner, activations, out_grads)
    return pl.pallas_call(
        kernel,
        name="kv_backward",
        out_shape=(
            jax.ShapeDtypeStruct((192, 1024), bf16),
            jax.ShapeDtypeStruct((1, CAP, BLK, BLK), f32),
        ),
        in_specs=[smem] + [any_space] * 3,
        out_specs=(vmem, vmem),
        scratch_shapes=[
            pltpu.VMEM((8, 1024, 256), bf16),
            pltpu.VMEM((64, 256), bf16),
            pltpu.VMEM((8, 192, 256), bf16),
            pltpu.VMEM((192, 1024), f32),
            pltpu.VMEM((NB, 64, BLK), f32),
            pltpu.VMEM((NB, 64, BLK), f32),
            pltpu.VMEM((NX, NB, 16, BLK), f32),
            pltpu.VMEM((NX, NB, 16, BLK), f32),
            pltpu.VMEM((PIECES, 8, BLK), f32),
            pltpu.VMEM((NZ, 8, BLK), f32),
            pltpu.VMEM((8, BLK), f32),
            pltpu.VMEM((PIECES, 8, BLK), f32),
            pltpu.VMEM((7, CAP, 16, BLK), f32),
            pltpu.VMEM((CAP, BLK, BLK), f32),
            dma((4,)), dma, dma, dma, dma, dma, dma, dma((5,)),
            dma((16,)), dma((8,)), dma((8,)), dma((8,)), dma((8,)), dma, dma((5,)),
        ],
        compiler_params=pltpu.CompilerParams(collective_id=0, has_side_effects=True),
    )(sel, part, out_grads, kv_weight)


def solution(mesh):
    return jax.shard_map(
        local,
        mesh=mesh,
        in_specs=(
            P("dp", None),
            P("dp", "tensor"),
            P("dp", "tensor"),
            P("tensor", None),
            P("tensor", None),
        ),
        out_specs=(P("dp", "tensor"), P("tensor", "dp", None, None)),
        check_vma=False,
    )
```

```python
import jax
import jax.numpy as jnp
from jax import lax
from jax.experimental import pallas as pl
from jax.experimental.pallas import tpu as pltpu
from jax.sharding import PartitionSpec as P

MESH = pl.DeviceIdType.MESH
NX, NY, NZ = 4, 8, 16
BLK = 128
NB = 6
CAP = 2
PIECES = 6
SCALE = 24576.0 ** -0.5


def block_terms(ids_ref, owner_ref, x_hbm, g_hbm, part_ref, sel_ref, xbuf, gbuf, sems):
    dp = lax.axis_index("dp")
    c, x, z = dp % 2, (dp // 2) % NX, dp // 8
    copies = [pltpu.make_async_copy(g_hbm, gbuf, sems.at[NB])]
    for n in range(NB):
        rows = pl.multiple_of((ids_ref[0, n] // 2) * BLK, BLK)
        copies.append(pltpu.make_async_copy(x_hbm.at[:, pl.ds(rows, BLK)], xbuf.at[n], sems.at[n]))
    for copy in copies:
        copy.start()
    owners = [owner_ref[0, n] for n in range(NB)]
    ranks = []
    for n in range(NB):
        r = jnp.int32(0)
        for m in range(n):
            r = r + (owners[m] == owners[n]).astype(jnp.int32)
        ranks.append(r)
    for i in range(8):
        to = (z * NX + (x + i // 2) % NX) * 2 + (c + i % 2) % 2
        for s in range(CAP):
            for n in range(NB):
                hit = (owners[n] == to) & (ranks[n] == s)
                sel_ref[0, (i * CAP + s) * NB + n] = jnp.where(hit, jnp.float32(1), jnp.float32(0))
    copies[0].wait()
    for n in range(NB):
        copies[n + 1].wait()
        gb = gbuf[:, pl.ds(pl.multiple_of((ids_ref[0, n] % 2) * BLK, BLK), BLK)]
        term = lax.dot_general(
            xbuf[n], gb, (((0,), (0,)), ((), ())), preferred_element_type=jnp.float32
        )
        part_ref[0, n] = term[:64]
        part_ref[1, n] = term[64:]


def kernel(
    sel_ref, part_hbm, g_hbm, w_hbm, out_ref, owned_ref,
    wbuf, wown, gbuf, acc, part, half, xsum, xrecv, zsum, zrecv, mine, full, pick, got,
    load_sem, shard_ss, zs, xs, rs, cs, gs, as_, zr, xr, xl, x2, cr, gr, ar,
):
    dp = lax.axis_index("dp")
    y = lax.axis_index("tensor")
    c = dp % 2
    x = (dp // 2) % NX
    z = dp // 8
    role = (z - 2 * y + NZ) % NZ
    hown = role % 2
    slab = role < 2
    piece = (role + 2) % NZ
    owner = piece < PIECES
    spot = jnp.minimum(piece, PIECES - 1)
    stop = (role == 3) | (role == 5) | (role == 7) | (role == 10) | (role == 12) | (role == 14)
    xp, xm, xo = (x + 1) % NX, (x + 3) % NX, (x + 2) % NX

    def dev(xx, yy, zz, cc):
        return ((zz * NX + xx) * 2 + cc, yy)

    def col(xx, hh, cc):
        return pl.multiple_of(hh * 512 + xx * 128 + cc * 64, 64)

    def unit(j, xx, hh, cc):
        return wbuf.at[j, pl.ds(col(xx, hh, cc), 64), :]

    def send(src, dst, ssem, rsem, to):
        pltpu.make_async_remote_copy(
            src_ref=src, dst_ref=dst, send_sem=ssem, recv_sem=rsem, device_id=to, device_id_type=MESH
        ).start()

    def desc(ref, ssem, rsem):
        return pltpu.make_async_remote_copy(
            src_ref=ref, dst_ref=ref, send_sem=ssem, recv_sem=rsem,
            device_id=dev(x, y, z, 1 - c), device_id_type=MESH,
        )

    def wait_recv(ref, rsem):
        desc(ref, cs, rsem).wait_recv()

    def wait_send(ref, ssem):
        desc(ref, ssem, gr).wait_send()

    load_p = pltpu.make_async_copy(part_hbm.at[c], part, load_sem.at[0])
    load_g = pltpu.make_async_copy(g_hbm, gbuf.at[y], load_sem.at[1])
    load_w = pltpu.make_async_copy(w_hbm, wown, load_sem.at[2])
    load_w.start()
    load_g.start()
    load_p.start()
    local_w = pltpu.make_async_copy(w_hbm, unit(0, x, hown, c), load_sem.at[3])

    @pl.when(slab)
    def _():
        local_w.start()

    barrier = pltpu.get_barrier_semaphore()
    peers = [dev(x, (y + i) % NY, z, c) for i in range(1, NY)]
    peers += [dev(x, y, (z + i) % NZ, c) for i in range(1, NZ)]
    peers += [dev((x + i) % NX, y, z, c) for i in range(1, NX)]
    peers += [dev((x + i) % NX, y, z, 1 - c) for i in range(NX)]
    for p in peers:
        pl.semaphore_signal(barrier, inc=1, device_id=p, device_id_type=MESH)

    load_g.wait()
    load_p.wait()
    load_w.wait()
    pl.semaphore_wait(barrier, len(peers))

    yd = z // 2
    d = (y - yd + NY) % NY
    jd = jnp.where(d == 0, 0, jnp.where(d <= 4, 2 * d - 1, 16 - 2 * d))

    @pl.when(jnp.logical_not(slab))
    def _():
        send(wown, unit(jd, x, hown, c), shard_ss, zr.at[2 * jd + z % 2], dev(x, yd, z, c))

    send(part_hbm.at[1 - c], half, as_.at[0], ar.at[0], dev(x, y, z, 1 - c))

    def spread(j, h):
        u = unit(j, x, h, c)
        k = 2 * j + h
        source = slab & (h == hown)
        up = jnp.where(role == 0, 3, jnp.where(role == 1, 2, jnp.where((role == 3) | (role == 5), 2, 1)))
        down = jnp.where(role == 0, 2, jnp.where(role == 1, 3, jnp.where((role == 12) | (role == 14), 2, 1)))
        go = source | stop

        @pl.when(go)
        def _():
            send(u, u, zs, zr.at[k], dev(x, y, (z + up) % NZ, c))
            send(u, u, zs, zr.at[k], dev(x, y, (z - down + NZ) % NZ, c))

        @pl.when(source)
        def _():
            other = jnp.where(role == 0, 1, NZ - 1)
            send(u, u, zs, zr.at[k], dev(x, y, (z + other) % NZ, c))

        send(u, u, xs, xr.at[j], dev(xp, y, z, c))
        send(u, u, xs, xl.at[j], dev(xm, y, z, c))
        send(u, u, cs, cr.at[j], dev(x, y, z, 1 - c))

    def take(j, h):
        wait_recv(unit(j, x, h, c), zr.at[2 * j + h])
        spread(j, h)

    def core_step():
        wait_recv(half, ar.at[0])
        s = part[...] + half[...]
        for i in range(NX):
            xsum[i] = s[:, 16 * i:16 * (i + 1), :]
        for i in range(1, NX):
            xx = (x + i) % NX
            send(xsum.at[xx], xrecv.at[x], as_.at[1], ar.at[1], dev(xx, y, z, c))
        xrecv[x] = xsum[x]

    def x_step():
        wait_recv(xrecv.at[pl.ds(0, 3)], ar.at[1])
        s = xrecv[0] + xrecv[1] + xrecv[2] + xrecv[3]
        zsum[...] = s

        def body(i, carry):
            @pl.when(i != piece)
            def _():
                to = (i + 14 + 2 * y) % NZ
                send(zsum.at[i], zrecv.at[z], as_.at[2], ar.at[2], dev(x, y, to, c))

            return carry

        lax.fori_loop(0, PIECES, body, 0)

    def z_step():
        zrecv[z] = zsum[spot]
        wait_recv(zrecv.at[pl.ds(0, NZ - 1)], ar.at[2])
        s = zrecv[0]
        for i in range(1, NZ):
            s = s + zrecv[i]
        mine[...] = s * SCALE
        full[spot] = s * SCALE

        def body(i, carry):
            zz = (z + i) % NZ
            send(mine, full.at[spot], as_.at[3], ar.at[3], dev(x, y, zz, c))
            return carry

        lax.fori_loop(1, NZ, body, 0)

    def send_g():
        for i in (1, 7, 2, 6, 3, 5, 4):
            send(gbuf.at[y], gbuf.at[y], gs, gr, dev(x, (y + i) % NY, z, c))

    @pl.when(slab)
    def _():
        local_w.wait()
        spread(0, hown)

        def body(j, carry):
            take(j, hown)
            return carry

        lax.fori_loop(1, 8, body, 0)
        core_step()
        take(0, 1 - hown)
        take(1, 1 - hown)
        x_step()
        send_g()

        def body2(j, carry):
            take(j, 1 - hown)
            return carry

        lax.fori_loop(2, 8, body2, 0)
        z_step()

    def units(start, stop_at):
        def body(j, carry):
            take(j, 0)
            take(j, 1)
            return carry

        lax.fori_loop(start, stop_at, body, 0)

    first = (role == 3) | (role == 14)

    @pl.when(first)
    def _():
        units(0, 3)
        core_step()
        units(3, 5)
        x_step()
        send_g()
        units(5, 8)
        z_step()

    side = (role == 2) | (role == 15)

    @pl.when(jnp.logical_not(slab | first))
    def _():
        core_step()
        x_step()
        send_g()
        units(0, 6)

        @pl.when(side)
        def _():
            z_step()

        units(6, 8)

    def body(j, carry):
        wait_recv(wbuf.at[j, pl.ds(0, 128), :], xr.at[j])
        even = j % 2 == 0
        for h in range(2):
            u = unit(j, xm, h, c)

            @pl.when(even)
            def _():
                send(u, u, rs, x2.at[j], dev(xp, y, z, c))

            send(u, u, cs, cr.at[j], dev(x, y, z, 1 - c))
        wait_recv(wbuf.at[j, pl.ds(0, 128), :], xl.at[j])
        for h in range(2):
            u = unit(j, xp, h, c)

            @pl.when(jnp.logical_not(even))
            def _():
                send(u, u, rs, x2.at[j], dev(xm, y, z, c))

            send(u, u, cs, cr.at[j], dev(x, y, z, 1 - c))
        return carry

    lax.fori_loop(0, 8, body, 0)

    def deliver():
        @pl.when(owner)
        def _():
            wait_recv(full.at[pl.ds(0, PIECES - 1)], ar.at[3])

        @pl.when(jnp.logical_not(owner))
        def _():
            wait_recv(full, ar.at[3])

        row0 = pl.multiple_of(c * 64 + x * 16, 16)
        for i in range(8):
            xx, cc = (x + i // 2) % NX, (c + i % 2) % 2
            to = (z * NX + xx) * 2 + cc
            for s in range(CAP):
                total = jnp.zeros((16, 128), jnp.float32)
                for n in range(NB):
                    total = total + full[n] * sel_ref[0, (i * CAP + s) * NB + n]
                if i == 0:
                    got[s, pl.ds(row0, 16), :] = total
                else:
                    pick[i - 1, s] = total
            if i > 0:
                send(pick.at[i - 1], got.at[:, pl.ds(row0, 16), :], as_.at[4], ar.at[4], (to, y))

    late = slab | (role == 3) | (role == 14)

    @pl.when(jnp.logical_not(late))
    def _():
        deliver()

    wait_recv(gbuf.at[pl.ds(0, 7)], gr)

    def product(j):
        shift = ((j + 1) // 2) * (2 * (j % 2) - 1)
        yw = (y + shift + NY) % NY
        wait_recv(wbuf.at[j, pl.ds(0, 512), :], cr.at[j])
        return lax.dot_general(
            gbuf[yw], wbuf[j], (((1,), (1,)), ((), ())), preferred_element_type=jnp.float32
        )

    def fetch(j):
        wait_recv(wbuf.at[j, pl.ds(0, 128), :], x2.at[j])
        for h in range(2):
            u = unit(j, xo, h, c)
            send(u, u, cs, cr.at[j], dev(x, y, z, 1 - c))

    acc[...] = jnp.zeros_like(acc)
    fetch(0)

    def body(j, carry):
        fetch(j)
        acc[...] += product(j - 1)
        return carry

    lax.fori_loop(1, 8, body, 0)
    out_ref[...] = (acc[...] + product(7)).astype(jnp.bfloat16)

    @pl.when(late)
    def _():
        deliver()

    wait_recv(got.at[:, pl.ds(0, 112), :], ar.at[4])
    owned_ref[0] = got[...]

    @pl.when(jnp.logical_not(slab))
    def _():
        wait_send(wown, shard_ss)

    @pl.when(slab)
    def _():
        wait_send(wbuf.at[pl.ds(0, 3), pl.ds(0, 512), :], zs)

    @pl.when(stop)
    def _():
        wait_send(wbuf.at[pl.ds(0, 2)], zs)

    wait_send(wbuf.at[pl.ds(0, 2)], xs)
    wait_send(wbuf.at[pl.ds(0, 1)], rs)
    wait_send(wbuf.at[pl.ds(0, 4)], cs)
    wait_send(gbuf.at[pl.ds(0, 7)], gs)
    wait_send(half, as_.at[0])
    wait_send(xsum.at[pl.ds(0, 3)], as_.at[1])

    @pl.when(owner)
    def _():
        wait_send(zsum.at[pl.ds(0, PIECES - 1)], as_.at[2])
        wait_send(zrecv.at[pl.ds(0, NZ - 1)], as_.at[3])

    @pl.when(jnp.logical_not(owner))
    def _():
        wait_send(zsum, as_.at[2])

    wait_send(pick, as_.at[4])


def write(a_ref, b_ref, out_ref, owned_ref, a, b, sems):
    rows = [pl.ds(48 * i, 48) for i in range(4)]
    first = [pltpu.make_async_copy(a_ref.at[r], a.at[r], sems.at[i]) for i, r in enumerate(rows)]
    first += [pltpu.make_async_copy(b_ref, b, sems.at[4])]
    last = [pltpu.make_async_copy(a.at[r], out_ref.at[r], sems.at[5 + i]) for i, r in enumerate(rows)]
    last += [pltpu.make_async_copy(b, owned_ref, sems.at[9])]
    for copy in first:
        copy.start()
    for one, two in zip(first, last):
        one.wait()
        two.start()
    for two in last:
        two.wait()


def local(activations, out_grads, kv_weight, block_ids, block_owner):
    f32, bf16 = jnp.float32, jnp.bfloat16
    dma = pltpu.SemaphoreType.DMA
    any_space = pl.BlockSpec(memory_space=pl.ANY)
    smem = pl.BlockSpec(memory_space=pltpu.SMEM)
    vmem = pl.BlockSpec(memory_space=pltpu.VMEM)
    part, sel = pl.pallas_call(
        block_terms,
        name="block_terms",
        out_shape=(
            jax.ShapeDtypeStruct((2, NB, 64, BLK), f32),
            jax.ShapeDtypeStruct((1, 8 * CAP * NB), f32),
        ),
        in_specs=[smem] * 2 + [any_space] * 2,
        out_specs=(vmem, smem),
        scratch_shapes=[
            pltpu.VMEM((NB, 192, BLK), bf16),
            pltpu.VMEM((192, 256), bf16),
            dma((NB + 1,)),
        ],
    )(block_ids, block_owner, activations, out_grads)
    result = pl.pallas_call(
        kernel,
        name="kv_backward",
        out_shape=(
            jax.ShapeDtypeStruct((192, 1024), bf16),
            jax.ShapeDtypeStruct((1, CAP, BLK, BLK), f32),
        ),
        in_specs=[smem] + [any_space] * 3,
        out_specs=(vmem, vmem),
        scratch_shapes=[
            pltpu.VMEM((8, 1024, 256), bf16),
            pltpu.VMEM((64, 256), bf16),
            pltpu.VMEM((8, 192, 256), bf16),
            pltpu.VMEM((192, 1024), f32),
            pltpu.VMEM((NB, 64, BLK), f32),
            pltpu.VMEM((NB, 64, BLK), f32),
            pltpu.VMEM((NX, NB, 16, BLK), f32),
            pltpu.VMEM((NX, NB, 16, BLK), f32),
            pltpu.VMEM((PIECES, 16, BLK), f32),
            pltpu.VMEM((NZ, 16, BLK), f32),
            pltpu.VMEM((16, BLK), f32),
            pltpu.VMEM((PIECES, 16, BLK), f32),
            pltpu.VMEM((7, CAP, 16, BLK), f32),
            pltpu.VMEM((CAP, BLK, BLK), f32),
            dma((4,)), dma, dma, dma, dma, dma, dma, dma((5,)),
            dma((16,)), dma((8,)), dma((8,)), dma((8,)), dma((8,)), dma, dma((5,)),
        ],
        compiler_params=pltpu.CompilerParams(collective_id=0, has_side_effects=True),
    )(sel, part, out_grads, kv_weight)
    return pl.pallas_call(
        write,
        name="write",
        out_shape=(
            jax.ShapeDtypeStruct((192, 1024), bf16),
            jax.ShapeDtypeStruct((1, CAP, BLK, BLK), f32),
        ),
        in_specs=[any_space] * 2,
        out_specs=(any_space, any_space),
        scratch_shapes=[
            pltpu.VMEM((192, 1024), bf16),
            pltpu.VMEM((1, CAP, BLK, BLK), f32),
            dma((10,)),
        ],
    )(*result)


def solution(mesh):
    return jax.shard_map(
        local,
        mesh=mesh,
        in_specs=(
            P("dp", None),
            P("dp", "tensor"),
            P("dp", "tensor"),
            P("tensor", None),
            P("tensor", None),
        ),
        out_specs=(P("dp", "tensor"), P("tensor", "dp", None, None)),
        check_vma=False,
    )
```

```python
import jax
import jax.numpy as jnp
from jax import lax
from jax.experimental import pallas as pl
from jax.experimental.pallas import tpu as pltpu
from jax.sharding import PartitionSpec as P

MESH = pl.DeviceIdType.MESH
NX, NY, NZ = 4, 8, 16
BLK = 128
NB = 6
CAP = 2
PIECES = 6
SCALE = 24576.0 ** -0.5


def block_terms(ids_ref, owner_ref, x_hbm, g_hbm, part_ref, sel_ref, xbuf, gbuf, sems):
    dp = lax.axis_index("dp")
    c, x, z = dp % 2, (dp // 2) % NX, dp // 8
    copies = [pltpu.make_async_copy(g_hbm, gbuf, sems.at[NB])]
    for n in range(NB):
        rows = pl.multiple_of((ids_ref[0, n] // 2) * BLK, BLK)
        copies.append(pltpu.make_async_copy(x_hbm.at[:, pl.ds(rows, BLK)], xbuf.at[n], sems.at[n]))
    for copy in copies:
        copy.start()
    owners = [owner_ref[0, n] for n in range(NB)]
    ranks = []
    for n in range(NB):
        r = jnp.int32(0)
        for m in range(n):
            r = r + (owners[m] == owners[n]).astype(jnp.int32)
        ranks.append(r)
    for i in range(8):
        to = (z * NX + (x + i // 2) % NX) * 2 + (c + i % 2) % 2
        for s in range(CAP):
            for n in range(NB):
                hit = (owners[n] == to) & (ranks[n] == s)
                sel_ref[0, (i * CAP + s) * NB + n] = jnp.where(hit, jnp.float32(1), jnp.float32(0))
    copies[0].wait()
    for n in range(NB):
        copies[n + 1].wait()
        gb = gbuf[:, pl.ds(pl.multiple_of((ids_ref[0, n] % 2) * BLK, BLK), BLK)]
        term = lax.dot_general(
            xbuf[n], gb, (((0,), (0,)), ((), ())), preferred_element_type=jnp.float32
        )
        part_ref[0, n] = term[:64]
        part_ref[1, n] = term[64:]


def kernel(
    sel_ref, part_hbm, g_hbm, w_hbm, out_ref, owned_ref,
    wbuf, wown, gbuf, acc, part, half, xsum, xrecv, zsum, zrecv, mine, full, pick, got,
    load_sem, shard_ss, zs, xs, rs, cs, gs, as_, hs, zr, xr, xl, x2, cr, gr, ar,
):
    dp = lax.axis_index("dp")
    y = lax.axis_index("tensor")
    c = dp % 2
    x = (dp // 2) % NX
    z = dp // 8
    role = (z - 2 * y + NZ) % NZ
    hown = role % 2
    slab = role < 2
    piece = (role + 2) % NZ
    owner = piece < PIECES
    spot = jnp.minimum(piece, PIECES - 1)
    stop = (role == 3) | (role == 5) | (role == 7) | (role == 10) | (role == 12) | (role == 14)
    xp, xm, xo = (x + 1) % NX, (x + 3) % NX, (x + 2) % NX

    def dev(xx, yy, zz, cc):
        return ((zz * NX + xx) * 2 + cc, yy)

    def col(xx, hh, cc):
        return pl.multiple_of(hh * 512 + xx * 128 + cc * 64, 64)

    def unit(j, xx, hh, cc):
        return wbuf.at[j, pl.ds(col(xx, hh, cc), 64), :]

    def send(src, dst, ssem, rsem, to):
        pltpu.make_async_remote_copy(
            src_ref=src, dst_ref=dst, send_sem=ssem, recv_sem=rsem, device_id=to, device_id_type=MESH
        ).start()

    def desc(ref, ssem, rsem):
        return pltpu.make_async_remote_copy(
            src_ref=ref, dst_ref=ref, send_sem=ssem, recv_sem=rsem,
            device_id=dev(x, y, z, 1 - c), device_id_type=MESH,
        )

    def wait_recv(ref, rsem):
        desc(ref, cs, rsem).wait_recv()

    def wait_send(ref, ssem):
        desc(ref, ssem, gr).wait_send()

    load_p = pltpu.make_async_copy(part_hbm.at[c], part, load_sem.at[0])
    load_g = pltpu.make_async_copy(g_hbm, gbuf.at[y], load_sem.at[1])
    load_w = pltpu.make_async_copy(w_hbm, wown, load_sem.at[2])
    load_w.start()
    load_g.start()
    load_p.start()
    local_w = pltpu.make_async_copy(w_hbm, unit(0, x, hown, c), load_sem.at[3])

    @pl.when(slab)
    def _():
        local_w.start()

    barrier = pltpu.get_barrier_semaphore()
    peers = [dev(x, (y + i) % NY, z, c) for i in range(1, NY)]
    peers += [dev(x, y, (z + i) % NZ, c) for i in (1, NZ - 1)]
    peers += [dev((x + i) % NX, y, z, c) for i in range(1, NX)]
    peers += [dev((x + i) % NX, y, z, 1 - c) for i in range(NX)]
    for p in peers:
        pl.semaphore_signal(barrier, inc=1, device_id=p, device_id_type=MESH)

    load_g.wait()
    load_p.wait()
    load_w.wait()

    def tell(sem, dz):
        pl.semaphore_signal(sem, inc=1, device_id=dev(x, y, (z + dz + NZ) % NZ, c), device_id_type=MESH)

    parent = jnp.where((role == 2) | (role == 4) | (role == 6), 1, jnp.where(
        (role == 5) | (role == 7), -2, jnp.where((role == 10) | (role == 12), 2, jnp.where(
            (role == 8) | (role == 11) | (role == 13) | (role == 15), -1, 1))))

    @pl.when(jnp.logical_not(slab | (role == 3) | (role == 14)))
    def _():
        tell(barrier, parent)

    @pl.when(role == 3)
    def _():
        tell(barrier, -3)
        tell(barrier, -2)

    @pl.when(role == 14)
    def _():
        tell(barrier, 2)
        tell(barrier, 3)

    pl.semaphore_wait(barrier, len(peers) + jnp.where(slab | stop, 2, 0))

    def told(n):
        pl.semaphore_wait(hs.at[n], 2)
        if n < 2:
            tell(hs.at[n + 1], 2 << n)
            tell(hs.at[n + 1], -(2 << n))

    tell(hs.at[0], 1)
    tell(hs.at[0], -1)

    yd = z // 2
    d = (y - yd + NY) % NY
    jd = jnp.where(d == 0, 0, jnp.where(d <= 4, 2 * d - 1, 16 - 2 * d))

    @pl.when(jnp.logical_not(slab))
    def _():
        send(wown, unit(jd, x, hown, c), shard_ss, zr.at[2 * jd + z % 2], dev(x, yd, z, c))

    send(part_hbm.at[1 - c], half, as_.at[0], ar.at[0], dev(x, y, z, 1 - c))

    def spread(j, h):
        u = unit(j, x, h, c)
        k = 2 * j + h
        source = slab & (h == hown)
        up = jnp.where(role == 0, 3, jnp.where(role == 1, 2, jnp.where((role == 3) | (role == 5), 2, 1)))
        down = jnp.where(role == 0, 2, jnp.where(role == 1, 3, jnp.where((role == 12) | (role == 14), 2, 1)))
        go = source | stop

        @pl.when(go)
        def _():
            send(u, u, zs, zr.at[k], dev(x, y, (z + up) % NZ, c))
            send(u, u, zs, zr.at[k], dev(x, y, (z - down + NZ) % NZ, c))

        @pl.when(source)
        def _():
            other = jnp.where(role == 0, 1, NZ - 1)
            send(u, u, zs, zr.at[k], dev(x, y, (z + other) % NZ, c))

        send(u, u, xs, xr.at[j], dev(xp, y, z, c))
        send(u, u, xs, xl.at[j], dev(xm, y, z, c))
        send(u, u, cs, cr.at[j], dev(x, y, z, 1 - c))

    def take(j, h):
        wait_recv(unit(j, x, h, c), zr.at[2 * j + h])
        spread(j, h)

    def core_step():
        wait_recv(half, ar.at[0])
        s = part[...] + half[...]
        for i in range(NX):
            xsum[i] = s[:, 16 * i:16 * (i + 1), :]
        for i in range(1, NX):
            xx = (x + i) % NX
            send(xsum.at[xx], xrecv.at[x], as_.at[1], ar.at[1], dev(xx, y, z, c))
        xrecv[x] = xsum[x]

    def x_step():
        wait_recv(xrecv.at[pl.ds(0, 3)], ar.at[1])
        s = xrecv[0] + xrecv[1] + xrecv[2] + xrecv[3]
        zsum[...] = s

    def out_step():
        told(2)

        def body(i, carry):
            @pl.when(i != piece)
            def _():
                to = (i + 14 + 2 * y) % NZ
                send(zsum.at[i], zrecv.at[z], as_.at[2], ar.at[2], dev(x, y, to, c))

            return carry

        lax.fori_loop(0, PIECES, body, 0)

    def z_step():
        zrecv[z] = zsum[spot]
        wait_recv(zrecv.at[pl.ds(0, NZ - 1)], ar.at[2])
        s = zrecv[0]
        for i in range(1, NZ):
            s = s + zrecv[i]
        mine[...] = s * SCALE
        full[spot] = s * SCALE

        def body(i, carry):
            zz = (z + i) % NZ
            send(mine, full.at[spot], as_.at[3], ar.at[3], dev(x, y, zz, c))
            return carry

        lax.fori_loop(1, NZ, body, 0)

    def send_g():
        for i in (1, 7, 2, 6, 3, 5, 4):
            send(gbuf.at[y], gbuf.at[y], gs, gr, dev(x, (y + i) % NY, z, c))

    @pl.when(slab)
    def _():
        local_w.wait()
        spread(0, hown)
        told(0)
        take(1, hown)
        told(1)

        def body(j, carry):
            take(j, hown)
            return carry

        lax.fori_loop(2, 8, body, 0)
        core_step()
        take(0, 1 - hown)
        take(1, 1 - hown)
        x_step()
        send_g()
        out_step()

        def body2(j, carry):
            take(j, 1 - hown)
            return carry

        lax.fori_loop(2, 8, body2, 0)
        z_step()

    def units(start, stop_at):
        def body(j, carry):
            take(j, 0)
            take(j, 1)
            return carry

        lax.fori_loop(start, stop_at, body, 0)

    first = (role == 3) | (role == 14)

    @pl.when(first)
    def _():
        told(0)
        units(0, 1)
        told(1)
        units(1, 3)
        core_step()
        units(3, 5)
        x_step()
        send_g()
        out_step()
        units(5, 8)
        z_step()

    side = (role == 2) | (role == 15)

    @pl.when(jnp.logical_not(slab | first))
    def _():
        told(0)
        core_step()
        told(1)
        x_step()
        out_step()
        send_g()
        units(0, 6)

        @pl.when(side)
        def _():
            z_step()

        units(6, 8)

    def body(j, carry):
        wait_recv(wbuf.at[j, pl.ds(0, 128), :], xr.at[j])
        even = j % 2 == 0
        for h in range(2):
            u = unit(j, xm, h, c)

            @pl.when(even)
            def _():
                send(u, u, rs, x2.at[j], dev(xp, y, z, c))

            send(u, u, cs, cr.at[j], dev(x, y, z, 1 - c))
        wait_recv(wbuf.at[j, pl.ds(0, 128), :], xl.at[j])
        for h in range(2):
            u = unit(j, xp, h, c)

            @pl.when(jnp.logical_not(even))
            def _():
                send(u, u, rs, x2.at[j], dev(xm, y, z, c))

            send(u, u, cs, cr.at[j], dev(x, y, z, 1 - c))
        return carry

    lax.fori_loop(0, 8, body, 0)

    def deliver():
        @pl.when(owner)
        def _():
            wait_recv(full.at[pl.ds(0, PIECES - 1)], ar.at[3])

        @pl.when(jnp.logical_not(owner))
        def _():
            wait_recv(full, ar.at[3])

        row0 = pl.multiple_of(c * 64 + x * 16, 16)
        for i in range(8):
            xx, cc = (x + i // 2) % NX, (c + i % 2) % 2
            to = (z * NX + xx) * 2 + cc
            for s in range(CAP):
                total = jnp.zeros((16, 128), jnp.float32)
                for n in range(NB):
                    total = total + full[n] * sel_ref[0, (i * CAP + s) * NB + n]
                if i == 0:
                    got[s, pl.ds(row0, 16), :] = total
                else:
                    pick[i - 1, s] = total
            if i > 0:
                send(pick.at[i - 1], got.at[:, pl.ds(row0, 16), :], as_.at[4], ar.at[4], (to, y))

    late = slab | (role == 3) | (role == 14)

    @pl.when(jnp.logical_not(late))
    def _():
        deliver()

    wait_recv(gbuf.at[pl.ds(0, 7)], gr)

    def product(j):
        shift = ((j + 1) // 2) * (2 * (j % 2) - 1)
        yw = (y + shift + NY) % NY
        wait_recv(wbuf.at[j, pl.ds(0, 512), :], cr.at[j])
        return lax.dot_general(
            gbuf[yw], wbuf[j], (((1,), (1,)), ((), ())), preferred_element_type=jnp.float32
        )

    def fetch(j):
        wait_recv(wbuf.at[j, pl.ds(0, 128), :], x2.at[j])
        for h in range(2):
            u = unit(j, xo, h, c)
            send(u, u, cs, cr.at[j], dev(x, y, z, 1 - c))

    acc[...] = jnp.zeros_like(acc)
    fetch(0)

    def body(j, carry):
        fetch(j)
        acc[...] += product(j - 1)
        return carry

    lax.fori_loop(1, 8, body, 0)
    out_ref[...] = (acc[...] + product(7)).astype(jnp.bfloat16)

    @pl.when(late)
    def _():
        deliver()

    wait_recv(got.at[:, pl.ds(0, 112), :], ar.at[4])
    owned_ref[0] = got[...]

    @pl.when(jnp.logical_not(slab))
    def _():
        wait_send(wown, shard_ss)

    @pl.when(slab)
    def _():
        wait_send(wbuf.at[pl.ds(0, 3), pl.ds(0, 512), :], zs)

    @pl.when(stop)
    def _():
        wait_send(wbuf.at[pl.ds(0, 2)], zs)

    wait_send(wbuf.at[pl.ds(0, 2)], xs)
    wait_send(wbuf.at[pl.ds(0, 1)], rs)
    wait_send(wbuf.at[pl.ds(0, 4)], cs)
    wait_send(gbuf.at[pl.ds(0, 7)], gs)
    wait_send(half, as_.at[0])
    wait_send(xsum.at[pl.ds(0, 3)], as_.at[1])

    @pl.when(owner)
    def _():
        wait_send(zsum.at[pl.ds(0, PIECES - 1)], as_.at[2])
        wait_send(zrecv.at[pl.ds(0, NZ - 1)], as_.at[3])

    @pl.when(jnp.logical_not(owner))
    def _():
        wait_send(zsum, as_.at[2])

    wait_send(pick, as_.at[4])


def write(a_ref, b_ref, out_ref, owned_ref, a, b, sems):
    rows = [pl.ds(48 * i, 48) for i in range(4)]
    first = [pltpu.make_async_copy(a_ref.at[r], a.at[r], sems.at[i]) for i, r in enumerate(rows)]
    first += [pltpu.make_async_copy(b_ref, b, sems.at[4])]
    last = [pltpu.make_async_copy(a.at[r], out_ref.at[r], sems.at[5 + i]) for i, r in enumerate(rows)]
    last += [pltpu.make_async_copy(b, owned_ref, sems.at[9])]
    for copy in first:
        copy.start()
    for one, two in zip(first, last):
        one.wait()
        two.start()
    for two in last:
        two.wait()


def local(activations, out_grads, kv_weight, block_ids, block_owner):
    f32, bf16 = jnp.float32, jnp.bfloat16
    dma = pltpu.SemaphoreType.DMA
    any_space = pl.BlockSpec(memory_space=pl.ANY)
    smem = pl.BlockSpec(memory_space=pltpu.SMEM)
    vmem = pl.BlockSpec(memory_space=pltpu.VMEM)
    part, sel = pl.pallas_call(
        block_terms,
        name="block_terms",
        out_shape=(
            jax.ShapeDtypeStruct((2, NB, 64, BLK), f32),
            jax.ShapeDtypeStruct((1, 8 * CAP * NB), f32),
        ),
        in_specs=[smem] * 2 + [any_space] * 2,
        out_specs=(vmem, smem),
        scratch_shapes=[
            pltpu.VMEM((NB, 192, BLK), bf16),
            pltpu.VMEM((192, 256), bf16),
            dma((NB + 1,)),
        ],
    )(block_ids, block_owner, activations, out_grads)
    result = pl.pallas_call(
        kernel,
        name="kv_backward",
        out_shape=(
            jax.ShapeDtypeStruct((192, 1024), bf16),
            jax.ShapeDtypeStruct((1, CAP, BLK, BLK), f32),
        ),
        in_specs=[smem] + [any_space] * 3,
        out_specs=(vmem, vmem),
        scratch_shapes=[
            pltpu.VMEM((8, 1024, 256), bf16),
            pltpu.VMEM((64, 256), bf16),
            pltpu.VMEM((8, 192, 256), bf16),
            pltpu.VMEM((192, 1024), f32),
            pltpu.VMEM((NB, 64, BLK), f32),
            pltpu.VMEM((NB, 64, BLK), f32),
            pltpu.VMEM((NX, NB, 16, BLK), f32),
            pltpu.VMEM((NX, NB, 16, BLK), f32),
            pltpu.VMEM((PIECES, 16, BLK), f32),
            pltpu.VMEM((NZ, 16, BLK), f32),
            pltpu.VMEM((16, BLK), f32),
            pltpu.VMEM((PIECES, 16, BLK), f32),
            pltpu.VMEM((7, CAP, 16, BLK), f32),
            pltpu.VMEM((CAP, BLK, BLK), f32),
            dma((4,)), dma, dma, dma, dma, dma, dma, dma((5,)), pltpu.SemaphoreType.REGULAR((3,)),
            dma((16,)), dma((8,)), dma((8,)), dma((8,)), dma((8,)), dma, dma((5,)),
        ],
        compiler_params=pltpu.CompilerParams(collective_id=0, has_side_effects=True),
    )(sel, part, out_grads, kv_weight)
    return pl.pallas_call(
        write,
        name="write",
        out_shape=(
            jax.ShapeDtypeStruct((192, 1024), bf16),
            jax.ShapeDtypeStruct((1, CAP, BLK, BLK), f32),
        ),
        in_specs=[any_space] * 2,
        out_specs=(any_space, any_space),
        scratch_shapes=[
            pltpu.VMEM((192, 1024), bf16),
            pltpu.VMEM((1, CAP, BLK, BLK), f32),
            dma((10,)),
        ],
    )(*result)


def solution(mesh):
    return jax.shard_map(
        local,
        mesh=mesh,
        in_specs=(
            P("dp", None),
            P("dp", "tensor"),
            P("dp", "tensor"),
            P("tensor", None),
            P("tensor", None),
        ),
        out_specs=(P("dp", "tensor"), P("tensor", "dp", None, None)),
        check_vma=False,
    )
```

```python
import jax
import jax.numpy as jnp
from jax import lax
from jax.experimental import pallas as pl
from jax.experimental.pallas import tpu as pltpu
from jax.sharding import PartitionSpec as P

MESH = pl.DeviceIdType.MESH
NX, NY, NZ = 4, 8, 16
BLK = 128
NB = 6
CAP = 2
PIECES = 6
SCALE = 24576.0 ** -0.5


def block_terms(ids_ref, owner_ref, x_hbm, g_hbm, part_ref, sel_ref, xbuf, gbuf, sems):
    dp = lax.axis_index("dp")
    c, x, z = dp % 2, (dp // 2) % NX, dp // 8
    copies = [pltpu.make_async_copy(g_hbm, gbuf, sems.at[NB])]
    for n in range(NB):
        rows = pl.multiple_of((ids_ref[0, n] // 2) * BLK, BLK)
        copies.append(pltpu.make_async_copy(x_hbm.at[:, pl.ds(rows, BLK)], xbuf.at[n], sems.at[n]))
    for copy in copies:
        copy.start()
    owners = [owner_ref[0, n] for n in range(NB)]
    ranks = []
    for n in range(NB):
        r = jnp.int32(0)
        for m in range(n):
            r = r + (owners[m] == owners[n]).astype(jnp.int32)
        ranks.append(r)
    for i in range(8):
        to = (z * NX + (x + i // 2) % NX) * 2 + (c + i % 2) % 2
        for s in range(CAP):
            for n in range(NB):
                hit = (owners[n] == to) & (ranks[n] == s)
                sel_ref[0, (i * CAP + s) * NB + n] = jnp.where(hit, jnp.float32(1), jnp.float32(0))
    copies[0].wait()
    for n in range(NB):
        copies[n + 1].wait()
        gb = gbuf[:, pl.ds(pl.multiple_of((ids_ref[0, n] % 2) * BLK, BLK), BLK)]
        term = lax.dot_general(
            xbuf[n], gb, (((0,), (0,)), ((), ())), preferred_element_type=jnp.float32
        )
        part_ref[0, n] = term[:64]
        part_ref[1, n] = term[64:]


def kernel(
    sel_ref, part_hbm, g_hbm, w_hbm, out_ref, owned_ref,
    wbuf, wown, gbuf, acc, part, half, xsum, xrecv, zsum, zrecv, mine, full, pick, got,
    load_sem, shard_ss, zs, xs, rs, cs, gs, as_, hs, zr, xr, xl, x2, cr, gr, ar,
):
    dp = lax.axis_index("dp")
    y = lax.axis_index("tensor")
    c = dp % 2
    x = (dp // 2) % NX
    z = dp // 8
    role = (z - 2 * y + NZ) % NZ
    hown = role % 2
    slab = role < 2
    piece = (role + 2) % NZ
    owner = piece < PIECES
    spot = jnp.minimum(piece, PIECES - 1)
    stop = (role == 3) | (role == 5) | (role == 7) | (role == 10) | (role == 12) | (role == 14)
    xp, xm, xo = (x + 1) % NX, (x + 3) % NX, (x + 2) % NX

    def dev(xx, yy, zz, cc):
        return ((zz * NX + xx) * 2 + cc, yy)

    def col(xx, hh, cc):
        return pl.multiple_of(hh * 512 + xx * 128 + cc * 64, 64)

    def unit(j, xx, hh, cc):
        return wbuf.at[j, pl.ds(col(xx, hh, cc), 64), :]

    def send(src, dst, ssem, rsem, to):
        pltpu.make_async_remote_copy(
            src_ref=src, dst_ref=dst, send_sem=ssem, recv_sem=rsem, device_id=to, device_id_type=MESH
        ).start()

    def desc(ref, ssem, rsem):
        return pltpu.make_async_remote_copy(
            src_ref=ref, dst_ref=ref, send_sem=ssem, recv_sem=rsem,
            device_id=dev(x, y, z, 1 - c), device_id_type=MESH,
        )

    def wait_recv(ref, rsem):
        desc(ref, cs, rsem).wait_recv()

    def wait_send(ref, ssem):
        desc(ref, ssem, gr).wait_send()

    load_p = pltpu.make_async_copy(part_hbm.at[c], part, load_sem.at[0])
    load_g = pltpu.make_async_copy(g_hbm, gbuf.at[y], load_sem.at[1])
    load_w = pltpu.make_async_copy(w_hbm, wown, load_sem.at[2])
    load_w.start()
    load_g.start()
    load_p.start()
    local_w = pltpu.make_async_copy(w_hbm, unit(0, x, hown, c), load_sem.at[3])

    @pl.when(slab)
    def _():
        local_w.start()

    barrier = pltpu.get_barrier_semaphore()
    peers = [dev(x, (y + i) % NY, z, c) for i in range(1, NY)]
    peers += [dev(x, y, (z + i) % NZ, c) for i in (1, NZ - 1)]
    peers += [dev((x + i) % NX, y, z, c) for i in range(1, NX)]
    peers += [dev((x + i) % NX, y, z, 1 - c) for i in range(NX)]
    for p in peers:
        pl.semaphore_signal(barrier, inc=1, device_id=p, device_id_type=MESH)

    load_g.wait()
    load_p.wait()
    load_w.wait()

    def tell(sem, dz):
        pl.semaphore_signal(sem, inc=1, device_id=dev(x, y, (z + dz + NZ) % NZ, c), device_id_type=MESH)

    parent = jnp.where((role == 2) | (role == 4) | (role == 6), 1, jnp.where(
        (role == 5) | (role == 7), -2, jnp.where((role == 10) | (role == 12), 2, jnp.where(
            (role == 8) | (role == 11) | (role == 13) | (role == 15), -1, 1))))

    @pl.when(jnp.logical_not(slab | (role == 3) | (role == 14)))
    def _():
        tell(barrier, parent)

    @pl.when(role == 3)
    def _():
        tell(barrier, -3)
        tell(barrier, -2)

    @pl.when(role == 14)
    def _():
        tell(barrier, 2)
        tell(barrier, 3)

    pl.semaphore_wait(barrier, len(peers) + jnp.where(slab | stop, 2, 0))

    def told(n):
        pl.semaphore_wait(hs.at[n], 2)
        if n < 2:
            tell(hs.at[n + 1], 2 << n)
            tell(hs.at[n + 1], -(2 << n))

    tell(hs.at[0], 1)
    tell(hs.at[0], -1)

    yd = z // 2
    d = (y - yd + NY) % NY
    jd = jnp.where(d == 0, 0, jnp.where(d <= 4, 2 * d - 1, 16 - 2 * d))

    @pl.when(jnp.logical_not(slab))
    def _():
        send(wown, unit(jd, x, hown, c), shard_ss, zr.at[2 * jd + z % 2], dev(x, yd, z, c))

    send(part_hbm.at[1 - c], half, as_.at[0], ar.at[0], dev(x, y, z, 1 - c))

    def spread(j, h):
        u = unit(j, x, h, c)
        k = 2 * j + h
        source = slab & (h == hown)
        up = jnp.where(role == 0, 3, jnp.where(role == 1, 2, jnp.where((role == 3) | (role == 5), 2, 1)))
        down = jnp.where(role == 0, 2, jnp.where(role == 1, 3, jnp.where((role == 12) | (role == 14), 2, 1)))
        go = source | stop

        @pl.when(go)
        def _():
            send(u, u, zs, zr.at[k], dev(x, y, (z + up) % NZ, c))
            send(u, u, zs, zr.at[k], dev(x, y, (z - down + NZ) % NZ, c))

        @pl.when(source)
        def _():
            other = jnp.where(role == 0, 1, NZ - 1)
            send(u, u, zs, zr.at[k], dev(x, y, (z + other) % NZ, c))

        send(u, u, xs, xr.at[j], dev(xp, y, z, c))
        send(u, u, xs, xl.at[j], dev(xm, y, z, c))
        send(u, u, cs, cr.at[j], dev(x, y, z, 1 - c))

    def take(j, h):
        wait_recv(unit(j, x, h, c), zr.at[2 * j + h])
        spread(j, h)

    def core_step():
        wait_recv(half, ar.at[0])
        s = part[...] + half[...]
        for i in range(NX):
            xsum[i] = s[:, 16 * i:16 * (i + 1), :]
        for i in range(1, NX):
            xx = (x + i) % NX
            send(xsum.at[xx], xrecv.at[x], as_.at[1], ar.at[1], dev(xx, y, z, c))
        xrecv[x] = xsum[x]

    def x_step():
        wait_recv(xrecv.at[pl.ds(0, 3)], ar.at[1])
        s = xrecv[0] + xrecv[1] + xrecv[2] + xrecv[3]
        zsum[...] = s

    def out_step():
        told(2)

        def body(i, carry):
            @pl.when(i != piece)
            def _():
                to = (i + 14 + 2 * y) % NZ
                send(zsum.at[i], zrecv.at[z], as_.at[2], ar.at[2], dev(x, y, to, c))

            return carry

        lax.fori_loop(0, PIECES, body, 0)

    def z_step():
        zrecv[z] = zsum[spot]
        wait_recv(zrecv.at[pl.ds(0, NZ - 1)], ar.at[2])
        s = zrecv[0]
        for i in range(1, NZ):
            s = s + zrecv[i]
        mine[...] = s * SCALE
        full[spot] = s * SCALE

        def body(i, carry):
            zz = (z + i) % NZ
            send(mine, full.at[spot], as_.at[3], ar.at[3], dev(x, y, zz, c))
            return carry

        lax.fori_loop(1, NZ, body, 0)

    def send_g():
        for i in (1, 7, 2, 6, 3, 5, 4):
            send(gbuf.at[y], gbuf.at[y], gs, gr, dev(x, (y + i) % NY, z, c))

    @pl.when(slab)
    def _():
        local_w.wait()
        spread(0, hown)
        told(0)
        take(1, hown)
        told(1)

        def body(j, carry):
            take(j, hown)
            return carry

        lax.fori_loop(2, 4, body, 0)
        core_step()
        lax.fori_loop(4, 7, body, 0)
        x_step()
        out_step()
        lax.fori_loop(7, 8, body, 0)
        send_g()
        take(0, 1 - hown)
        take(1, 1 - hown)

        def body2(j, carry):
            take(j, 1 - hown)
            return carry

        lax.fori_loop(2, 8, body2, 0)
        z_step()

    def units(start, stop_at):
        def body(j, carry):
            take(j, 0)
            take(j, 1)
            return carry

        lax.fori_loop(start, stop_at, body, 0)

    first = (role == 3) | (role == 14)

    @pl.when(first)
    def _():
        told(0)
        units(0, 1)
        told(1)
        units(1, 3)
        core_step()
        units(3, 5)
        x_step()
        send_g()
        out_step()
        units(5, 8)
        z_step()

    side = (role == 2) | (role == 15)

    @pl.when(jnp.logical_not(slab | first))
    def _():
        told(0)
        core_step()
        told(1)
        x_step()
        out_step()
        send_g()
        units(0, 6)

        @pl.when(side)
        def _():
            z_step()

        units(6, 8)

    def body(j, carry):
        wait_recv(wbuf.at[j, pl.ds(0, 128), :], xr.at[j])
        even = j % 2 == 0
        for h in range(2):
            u = unit(j, xm, h, c)

            @pl.when(even)
            def _():
                send(u, u, rs, x2.at[j], dev(xp, y, z, c))

            send(u, u, cs, cr.at[j], dev(x, y, z, 1 - c))
        wait_recv(wbuf.at[j, pl.ds(0, 128), :], xl.at[j])
        for h in range(2):
            u = unit(j, xp, h, c)

            @pl.when(jnp.logical_not(even))
            def _():
                send(u, u, rs, x2.at[j], dev(xm, y, z, c))

            send(u, u, cs, cr.at[j], dev(x, y, z, 1 - c))
        return carry

    lax.fori_loop(0, 8, body, 0)

    def deliver():
        @pl.when(owner)
        def _():
            wait_recv(full.at[pl.ds(0, PIECES - 1)], ar.at[3])

        @pl.when(jnp.logical_not(owner))
        def _():
            wait_recv(full, ar.at[3])

        row0 = pl.multiple_of(c * 64 + x * 16, 16)
        for i in range(8):
            xx, cc = (x + i // 2) % NX, (c + i % 2) % 2
            to = (z * NX + xx) * 2 + cc
            for s in range(CAP):
                total = jnp.zeros((16, 128), jnp.float32)
                for n in range(NB):
                    total = total + full[n] * sel_ref[0, (i * CAP + s) * NB + n]
                if i == 0:
                    got[s, pl.ds(row0, 16), :] = total
                else:
                    pick[i - 1, s] = total
            if i > 0:
                send(pick.at[i - 1], got.at[:, pl.ds(row0, 16), :], as_.at[4], ar.at[4], (to, y))

    late = slab | (role == 3) | (role == 14)

    @pl.when(jnp.logical_not(late))
    def _():
        deliver()

    wait_recv(gbuf.at[pl.ds(0, 7)], gr)

    def product(j):
        shift = ((j + 1) // 2) * (2 * (j % 2) - 1)
        yw = (y + shift + NY) % NY
        wait_recv(wbuf.at[j, pl.ds(0, 512), :], cr.at[j])
        return lax.dot_general(
            gbuf[yw], wbuf[j], (((1,), (1,)), ((), ())), preferred_element_type=jnp.float32
        )

    def fetch(j):
        wait_recv(wbuf.at[j, pl.ds(0, 128), :], x2.at[j])
        for h in range(2):
            u = unit(j, xo, h, c)
            send(u, u, cs, cr.at[j], dev(x, y, z, 1 - c))

    acc[...] = jnp.zeros_like(acc)
    fetch(0)

    def body(j, carry):
        fetch(j)
        acc[...] += product(j - 1)
        return carry

    lax.fori_loop(1, 8, body, 0)
    out_ref[...] = (acc[...] + product(7)).astype(jnp.bfloat16)

    @pl.when(late)
    def _():
        deliver()

    wait_recv(got.at[:, pl.ds(0, 112), :], ar.at[4])
    owned_ref[0] = got[...]

    @pl.when(jnp.logical_not(slab))
    def _():
        wait_send(wown, shard_ss)

    @pl.when(slab)
    def _():
        wait_send(wbuf.at[pl.ds(0, 3), pl.ds(0, 512), :], zs)

    @pl.when(stop)
    def _():
        wait_send(wbuf.at[pl.ds(0, 2)], zs)

    wait_send(wbuf.at[pl.ds(0, 2)], xs)
    wait_send(wbuf.at[pl.ds(0, 1)], rs)
    wait_send(wbuf.at[pl.ds(0, 4)], cs)
    wait_send(gbuf.at[pl.ds(0, 7)], gs)
    wait_send(half, as_.at[0])
    wait_send(xsum.at[pl.ds(0, 3)], as_.at[1])

    @pl.when(owner)
    def _():
        wait_send(zsum.at[pl.ds(0, PIECES - 1)], as_.at[2])
        wait_send(zrecv.at[pl.ds(0, NZ - 1)], as_.at[3])

    @pl.when(jnp.logical_not(owner))
    def _():
        wait_send(zsum, as_.at[2])

    wait_send(pick, as_.at[4])


def write(a_ref, b_ref, out_ref, owned_ref, a, b, sems):
    rows = [pl.ds(48 * i, 48) for i in range(4)]
    first = [pltpu.make_async_copy(a_ref.at[r], a.at[r], sems.at[i]) for i, r in enumerate(rows)]
    first += [pltpu.make_async_copy(b_ref, b, sems.at[4])]
    last = [pltpu.make_async_copy(a.at[r], out_ref.at[r], sems.at[5 + i]) for i, r in enumerate(rows)]
    last += [pltpu.make_async_copy(b, owned_ref, sems.at[9])]
    for copy in first:
        copy.start()
    for one, two in zip(first, last):
        one.wait()
        two.start()
    for two in last:
        two.wait()


def local(activations, out_grads, kv_weight, block_ids, block_owner):
    f32, bf16 = jnp.float32, jnp.bfloat16
    dma = pltpu.SemaphoreType.DMA
    any_space = pl.BlockSpec(memory_space=pl.ANY)
    smem = pl.BlockSpec(memory_space=pltpu.SMEM)
    vmem = pl.BlockSpec(memory_space=pltpu.VMEM)
    part, sel = pl.pallas_call(
        block_terms,
        name="block_terms",
        out_shape=(
            jax.ShapeDtypeStruct((2, NB, 64, BLK), f32),
            jax.ShapeDtypeStruct((1, 8 * CAP * NB), f32),
        ),
        in_specs=[smem] * 2 + [any_space] * 2,
        out_specs=(vmem, smem),
        scratch_shapes=[
            pltpu.VMEM((NB, 192, BLK), bf16),
            pltpu.VMEM((192, 256), bf16),
            dma((NB + 1,)),
        ],
    )(block_ids, block_owner, activations, out_grads)
    result = pl.pallas_call(
        kernel,
        name="kv_backward",
        out_shape=(
            jax.ShapeDtypeStruct((192, 1024), bf16),
            jax.ShapeDtypeStruct((1, CAP, BLK, BLK), f32),
        ),
        in_specs=[smem] + [any_space] * 3,
        out_specs=(vmem, vmem),
        scratch_shapes=[
            pltpu.VMEM((8, 1024, 256), bf16),
            pltpu.VMEM((64, 256), bf16),
            pltpu.VMEM((8, 192, 256), bf16),
            pltpu.VMEM((192, 1024), f32),
            pltpu.VMEM((NB, 64, BLK), f32),
            pltpu.VMEM((NB, 64, BLK), f32),
            pltpu.VMEM((NX, NB, 16, BLK), f32),
            pltpu.VMEM((NX, NB, 16, BLK), f32),
            pltpu.VMEM((PIECES, 16, BLK), f32),
            pltpu.VMEM((NZ, 16, BLK), f32),
            pltpu.VMEM((16, BLK), f32),
            pltpu.VMEM((PIECES, 16, BLK), f32),
            pltpu.VMEM((7, CAP, 16, BLK), f32),
            pltpu.VMEM((CAP, BLK, BLK), f32),
            dma((4,)), dma, dma, dma, dma, dma, dma, dma((5,)), pltpu.SemaphoreType.REGULAR((3,)),
            dma((16,)), dma((8,)), dma((8,)), dma((8,)), dma((8,)), dma, dma((5,)),
        ],
        compiler_params=pltpu.CompilerParams(collective_id=0, has_side_effects=True),
    )(sel, part, out_grads, kv_weight)
    return pl.pallas_call(
        write,
        name="write",
        out_shape=(
            jax.ShapeDtypeStruct((192, 1024), bf16),
            jax.ShapeDtypeStruct((1, CAP, BLK, BLK), f32),
        ),
        in_specs=[any_space] * 2,
        out_specs=(any_space, any_space),
        scratch_shapes=[
            pltpu.VMEM((192, 1024), bf16),
            pltpu.VMEM((1, CAP, BLK, BLK), f32),
            dma((10,)),
        ],
    )(*result)


def solution(mesh):
    return jax.shard_map(
        local,
        mesh=mesh,
        in_specs=(
            P("dp", None),
            P("dp", "tensor"),
            P("dp", "tensor"),
            P("tensor", None),
            P("tensor", None),
        ),
        out_specs=(P("dp", "tensor"), P("tensor", "dp", None, None)),
        check_vma=False,
    )
```
